32 devices in a mesh: dp: 16 (over z, y, core), fsdp: 2 (over x).
Axes of the slice: x: 2, y: 2, z: 4, core: 2. Of those that a mesh axis runs over, the one named last changes fastest.
Arguments:
- inputs: bfloat16 [32, 1024, 768], P(('dp', 'fsdp')), may hold values from -6 to 6
- segments: int32 [32, 1024], P(('dp', 'fsdp')), may hold values from 0 to 7, never falling along the last dimension, each value on 1 to 512 neighbouring positions
- cotangent: bfloat16 [32, 1024, 768], P(('dp', 'fsdp')), may hold values from -6 to 6
- query_key_value_weight: bfloat16 [3, 768, 768], P(None, ('dp', 'fsdp')), may hold values from -0.21875 to 0.21875
- attention_out_weight: bfloat16 [768, 768], P(('dp', 'fsdp')), may hold values from -0.625 to 0.625
- feedforward_in_weight: bfloat16 [768, 3072], P(('dp', 'fsdp')), may hold values from -0.21875 to 0.21875
- feedforward_out_weight: bfloat16 [3072, 768], P(('dp', 'fsdp')), may hold values from -0.109375 to 0.109375
- projection_bias: float32 [4, 768], replicated, may hold values from -3 to 3
- hidden_unit_bias: float32 [3072], replicated, may hold values from -3 to 3
- norm_gain_rows: float32 [2, 768], replicated, may hold values from 0.25 to 1.75
- norm_shift_rows: float32 [2, 768], replicated, may hold values from -2 to 2
- adapter_down_factors: float32 [2, 768, 8], replicated, may hold values from -0.21875 to 0.21875
- adapter_up_factors: float32 [2, 8, 768], replicated, may hold values from -1.5 to 1.5
- down_first_moment: float32 [2, 768, 8], replicated, may hold values from -0.0038273276 to 0.0038273276
- up_first_moment: float32 [2, 8, 768], replicated, may hold values from -0.00057409913 to 0.00057409913
- down_second_moment: float32 [2, 768, 8], replicated, may hold values from 4.0690104e-08 to 6.5104166e-07
- up_second_moment: float32 [2, 8, 768], replicated, may hold values from 8.138021e-10 to 1.3020833e-08
- optimizer_step_count: int32 [1], replicated, may hold values from 1 to 20
Outputs:
- outputs: bfloat16 [32, 1024, 768], P(('dp', 'fsdp'))
- grad_inputs: float32 [32, 1024, 768], P(('dp', 'fsdp'))
- grad_norm: float32 [], replicated
- revised_down: float32 [2, 768, 8], replicated
- revised_up: float32 [2, 8, 768], replicated
- fresh_down_moment: float32 [2, 768, 8], replicated
- fresh_up_moment: float32 [2, 8, 768], replicated
- fresh_down_square: float32 [2, 768, 8], replicated
- fresh_up_square: float32 [2, 8, 768], replicated
The draws below stay inside these ranges and needn't reach their ends.
Inputs may be any that keep to these rules, and one draw needn't show every extreme that they name: `segments`: ids never fall along a pack; each segment holds 1 to 512 tokens, and some segment of each draw exactly that many.
All inputs are finite; a program needn't handle non-finite values.
Results may differ from the reference program's by a relative error of at most 0.013.
The reference program's roundings to bfloat16 on the way count: a program that leaves them out, or rounds other values in their place, can miss the bound.
Values may be sent and summed in bfloat16 or wider, within the bound.
No kernel may reach another device: no remote copies, remote signals or barrier semaphores. Data moves between devices by JAX's collectives and lax.ppermute only.
A program may use at most 256 MiB of HBM per device.

```python
import math
import jax
import jax.numpy as jnp
import numpy as np
from jax import lax

MODEL_SIZE = 768
HEAD_DIM = 64
FF = 3072
ADAPTER_RANK = 8
PACK_LEN = 1024
PACKS = 32
DOCUMENTS = 8


def levels(stream_key, shape, cuts, least, high):
    factor_of, own = 1.0, jax.random.fold_in(stream_key, 6)
    for dim, blocks in cuts:
        draws = jnp.exp(jax.random.uniform(jax.random.fold_in(own, dim), (blocks,), jnp.float32, least / len(cuts), high / len(cuts)))
        factor_of = factor_of * jnp.repeat(draws, shape[dim] // blocks).reshape([-1 if axis == dim else 1 for axis in range(len(shape))])
    return factor_of


def split_up(amount, total, most, lean):
    loads = [(1 << 20) // math.isqrt(grade ** lean) + 1 for grade in range(2, amount + 1)]
    spare, holding = total - most - (amount - 1), [1] * (amount - 1)
    while spare > 0:
        movable = [i for i in range(amount - 1) if holding[i] < most]
        pool, remaining = sum([loads[i] for i in movable]), spare
        for i in movable:
            addition = min(most - holding[i], max(1, remaining * loads[i] // pool), spare)
            holding[i] = holding[i] + addition
            spare = spare - addition
    return np.array([most] + holding)


def ragged_sizes(stream_key, number_of, total, bound, lean):
    if number_of == 2:
        one = jax.random.randint(stream_key, (), max(1, total - bound), min(bound, total - 1) + 1)
        return jnp.stack([one, total - one])
    tallies = jnp.asarray(split_up(number_of, total, bound, lean), jnp.int32)
    couples = (number_of - 1) // 2
    donor, receiver = tallies[1:1 + 2 * couples:2], tallies[2:2 + 2 * couples:2]
    margin = jnp.minimum(donor - 1, bound - receiver)
    moved = jax.random.randint(jax.random.fold_in(stream_key, 1), (couples,), 0, 1 << 20) % (margin + 1)
    tallies = tallies.at[1:1 + 2 * couples:2].set(donor - moved).at[2:2 + 2 * couples:2].set(receiver + moved)
    return tallies[jax.random.permutation(jax.random.fold_in(stream_key, 2), number_of)]


def normal_values(key, shape, deviation, reach, cuts=(), dtype=jnp.bfloat16):
    drawn = jax.random.normal(key, shape, jnp.float32) * deviation
    if len(cuts) > 0:
        drawn = levels(key, shape, cuts, -0.22, 0.18) * drawn
    return jnp.clip(drawn, min=-reach, max=reach).astype(dtype)


def setup_inputs(seed: int = 0) -> dict:
    arg_keys = jax.random.split(jax.random.key(seed), 19)
    return {
        "inputs": normal_values(arg_keys[0], (PACKS, PACK_LEN, MODEL_SIZE), 1.0, 6.0, ((0, 32),)),
        "segments": jax.vmap(lambda own: jnp.searchsorted(jnp.cumsum(ragged_sizes(own, DOCUMENTS, PACK_LEN, PACK_LEN // 2, 1)), jnp.arange(PACK_LEN), side="right"))(jax.random.split(arg_keys[1], PACKS)).reshape((PACKS, PACK_LEN)).astype(jnp.int32),
        "cotangent": normal_values(arg_keys[2], (PACKS, PACK_LEN, MODEL_SIZE), 1.0, 6.0, ((0, 32),)),
        "query_key_value_weight": normal_values(arg_keys[3], (3, MODEL_SIZE, MODEL_SIZE), MODEL_SIZE ** -0.5, 0.21875, ((1, 32),)),
        "attention_out_weight": normal_values(arg_keys[4], (MODEL_SIZE, MODEL_SIZE), (MODEL_SIZE // 8) ** -0.5, 0.625, ((0, 32),)),
        "feedforward_in_weight": normal_values(arg_keys[5], (MODEL_SIZE, FF), MODEL_SIZE ** -0.5, 0.21875, ((0, 32),)),
        "feedforward_out_weight": normal_values(arg_keys[6], (FF, MODEL_SIZE), FF ** -0.5, 0.109375, ((0, 32),)),
        "projection_bias": normal_values(arg_keys[7], (4, MODEL_SIZE), 0.5, 3.0, (), jnp.float32),
        "hidden_unit_bias": normal_values(arg_keys[8], (FF,), 0.5, 3.0, (), jnp.float32),
        "norm_gain_rows": jnp.clip(1.0 + 0.15 * jax.random.normal(arg_keys[9], (2, MODEL_SIZE), jnp.float32), 0.25, 1.75),
        "norm_shift_rows": normal_values(arg_keys[10], (2, MODEL_SIZE), 0.3, 2.0, (), jnp.float32),
        "adapter_down_factors": normal_values(arg_keys[11], (2, MODEL_SIZE, ADAPTER_RANK), MODEL_SIZE ** -0.5, 0.21875, (), jnp.float32),
        "adapter_up_factors": normal_values(arg_keys[12], (2, ADAPTER_RANK, MODEL_SIZE), 0.25, 1.5, (), jnp.float32),
        "down_first_moment": normal_values(arg_keys[13], (2, MODEL_SIZE, ADAPTER_RANK), (0.15 / (4 * MODEL_SIZE * ADAPTER_RANK) ** 0.5), 0.0038273276, (), jnp.float32),
        "up_first_moment": normal_values(arg_keys[14], (2, ADAPTER_RANK, MODEL_SIZE), (0.022 / (4 * MODEL_SIZE * ADAPTER_RANK) ** 0.5), 0.00057409913, (), jnp.float32),
        "down_second_moment": jnp.clip(jnp.exp(jax.random.uniform(arg_keys[15], (2, MODEL_SIZE, ADAPTER_RANK), jnp.float32, math.log(4.069010373086712e-08), math.log(6.51041659693874e-07))), 4.069010373086712e-08, 6.51041659693874e-07),
        "up_second_moment": jnp.clip(jnp.exp(jax.random.uniform(arg_keys[16], (2, ADAPTER_RANK, MODEL_SIZE), jnp.float32, math.log(8.138020812786806e-10), math.log(1.302083330045889e-08))), 8.138020812786806e-10, 1.302083330045889e-08),
        "optimizer_step_count": jax.random.randint(arg_keys[17], (1,), 1, 21).astype(jnp.int32),
    }


@jax.custom_vjp
def low(v):
    return lax.optimization_barrier(v.astype(jnp.bfloat16)).astype(jnp.float32)

@jax.custom_vjp
def low_back(v):
    return v

def low_keep(v):
    return (low(v), None)

def low_pass(kept, grad):
    return (grad,)

def back_keep(v):
    return (v, None)

def back_low(kept, grad):
    return (low(grad),)
low.defvjp(low_keep, low_pass)
low_back.defvjp(back_keep, back_low)
highest = lax.Precision.HIGHEST
ln_eps = 1e-05
adapter_alpha = 16.0
clip_max = 1.0
beta_one = 0.9
beta_two = 0.999
adam_eps = 1e-08
down_learning_rate = 0.02
up_learning_rate = 0.32
down_decay_factor = 0.1
up_decay_factor = 0.01
mask_fill = -1000000000.0

def matmul(left, right):
    return jnp.dot(left, right, precision=highest, preferred_element_type=jnp.float32)

def layer_norm(pre_values, gain_row, shift_row):
    average = lax.optimization_barrier(jnp.mean(pre_values, axis=-1, keepdims=True))
    centered = pre_values - average
    variance = lax.optimization_barrier(jnp.mean(centered * centered, axis=-1, keepdims=True))
    return centered * lax.rsqrt(variance + ln_eps) * gain_row + shift_row

def gelu_exact(pre_values):
    return jax.nn.gelu(pre_values, approximate=False)

def pack_forward(token_rows, segment, frozen, down_projected, up_proj):
    attn_full, output_full, expand_full, reduce_full, projection_bias, hidden_unit_bias, norm_gain_rows, norm_shift_rows = frozen
    length = token_rows.shape[0]
    model_width = token_rows.shape[1]
    head_count = model_width // HEAD_DIM
    adapter_scale = adapter_alpha / down_projected.shape[-1]
    down_reduced = low(down_projected)
    up_low = low(up_proj)
    query_down = low(low_back(matmul(token_rows, down_reduced[0])))
    value_down = low(low_back(matmul(token_rows, down_reduced[1])))
    queries = low(low_back(matmul(token_rows, attn_full[0]) + projection_bias[0] + adapter_scale * matmul(query_down, up_low[0])))
    key_rows = low(low_back(matmul(token_rows, attn_full[1])))
    values = low(low_back(matmul(token_rows, attn_full[2]) + projection_bias[1] + adapter_scale * matmul(value_down, up_low[1])))
    query_heads = queries.reshape(length, head_count, HEAD_DIM)
    key_heads = key_rows.reshape(length, head_count, HEAD_DIM)
    value_heads = values.reshape(length, head_count, HEAD_DIM)
    scores = jnp.einsum('qhd,khd->hqk', query_heads, key_heads, precision=highest) * HEAD_DIM ** (-0.5)
    scores = low_back(scores)
    same_doc = segment[:, None] == segment[None, :]
    masked = jnp.where(same_doc[None], scores, mask_fill)
    soft_weights = low(jax.nn.softmax(masked, axis=-1))
    attended = jnp.einsum('hqk,khd->qhd', soft_weights, value_heads, precision=highest).reshape(length, model_width)
    attended = low(low_back(attended))
    branch = low_back(matmul(attended, output_full) + projection_bias[2])
    normed_first = layer_norm(token_rows + branch, norm_gain_rows[0], norm_shift_rows[0])
    hidden = low_back(matmul(low(normed_first), expand_full) + hidden_unit_bias)
    active = low(gelu_exact(hidden))
    ffn_branch = low_back(matmul(active, reduce_full) + projection_bias[3])
    return layer_norm(normed_first + ffn_branch, norm_gain_rows[1], norm_shift_rows[1])

def adamw_update(weight_old, gradient, first_old, second_old, finished_steps, step_rate, decay_rate):
    first_new = beta_one * first_old + (1.0 - beta_one) * gradient
    second_new = beta_two * second_old + (1.0 - beta_two) * gradient * gradient
    first_hat = first_new / (1.0 - jnp.power(beta_one, finished_steps))
    second_hat = second_new / (1.0 - jnp.power(beta_two, finished_steps))
    weight_new = weight_old - step_rate * (first_hat / (jnp.sqrt(second_hat) + adam_eps) + decay_rate * weight_old)
    return (weight_new, first_new, second_new)

def reference(inputs, segments, cotangent, query_key_value_weight, attention_out_weight, feedforward_in_weight, feedforward_out_weight, projection_bias, hidden_unit_bias, norm_gain_rows, norm_shift_rows, adapter_down_factors, adapter_up_factors, down_first_moment, up_first_moment, down_second_moment, up_second_moment, optimizer_step_count):
    frozen = (query_key_value_weight.astype(jnp.float32), attention_out_weight.astype(jnp.float32), feedforward_in_weight.astype(jnp.float32), feedforward_out_weight.astype(jnp.float32), projection_bias, hidden_unit_bias, norm_gain_rows, norm_shift_rows)

    def one_pack(running, slices):
        token_rows, segment, pack_cot = slices

        def layer_forward(token_values, down_projected, up_proj):
            return pack_forward(token_values, segment, frozen, down_projected, up_proj)
        final_output, backward_map = jax.vjp(layer_forward, token_rows.astype(jnp.float32), adapter_down_factors, adapter_up_factors)
        grad_tokens, grad_down, grad_up = backward_map(pack_cot.astype(jnp.float32))
        return ((running[0] + grad_down, running[1] + grad_up), (final_output.astype(jnp.bfloat16), grad_tokens))
    starting = (jnp.zeros(adapter_down_factors.shape, jnp.float32), jnp.zeros(adapter_up_factors.shape, jnp.float32))
    (down_gradient_sum, up_gradient_sum), (outputs, grad_inputs) = lax.scan(one_pack, starting, (inputs, segments, cotangent))
    squares = jnp.sum(down_gradient_sum * down_gradient_sum) + jnp.sum(up_gradient_sum * up_gradient_sum)
    grad_norm = jnp.sqrt(squares)
    multiplier = jnp.minimum(1.0, clip_max / (grad_norm + 1e-06))
    finished_steps = optimizer_step_count[0].astype(jnp.float32)
    revised_down, fresh_down_moment, fresh_down_square = adamw_update(adapter_down_factors, down_gradient_sum * multiplier, down_first_moment, down_second_moment, finished_steps, down_learning_rate, down_decay_factor)
    revised_up, fresh_up_moment, fresh_up_square = adamw_update(adapter_up_factors, up_gradient_sum * multiplier, up_first_moment, up_second_moment, finished_steps, up_learning_rate, up_decay_factor)
    return (outputs, grad_inputs, grad_norm, revised_down, revised_up, fresh_down_moment, fresh_up_moment, fresh_down_square, fresh_up_square)
```

```python
import functools

import jax
import jax.numpy as jnp
from jax import lax
from jax.sharding import PartitionSpec as P

HEAD_DIM = 64


ln_eps = 1e-05
adapter_alpha = 16.0
clip_max = 1.0
beta_one = 0.9
beta_two = 0.999
adam_eps = 1e-08
down_learning_rate = 0.02
up_learning_rate = 0.32
down_decay_factor = 0.1
up_decay_factor = 0.01
mask_fill = -1000000000.0
block_rows = 512


def matmul(left, right):
    return jnp.dot(left, right, preferred_element_type=jnp.float32)


def layer_norm(pre_values, gain_row, shift_row):
    average = jnp.mean(pre_values, axis=-1, keepdims=True)
    centered = pre_values - average
    variance = jnp.mean(centered * centered, axis=-1, keepdims=True)
    return centered * lax.rsqrt(variance + ln_eps) * gain_row + shift_row


def gelu_exact(pre_values):
    return jax.nn.gelu(pre_values, approximate=False)


def adamw_update(
    weight_old, gradient, first_old, second_old, finished_steps, step_rate, decay_rate
):
    first_new = beta_one * first_old + (1.0 - beta_one) * gradient
    second_new = beta_two * second_old + (1.0 - beta_two) * gradient * gradient
    first_hat = first_new / (1.0 - jnp.power(beta_one, finished_steps))
    second_hat = second_new / (1.0 - jnp.power(beta_two, finished_steps))
    weight_new = weight_old - step_rate * (
        first_hat / (jnp.sqrt(second_hat) + adam_eps) + decay_rate * weight_old
    )
    return (weight_new, first_new, second_new)


def attention_forward(queries, key_rows, values, segment, head_dim):
    length, model_width = queries.shape
    head_count = model_width // head_dim
    block_size = min(block_rows, length)
    score_scale = float(head_dim) ** (-0.5)
    key_heads = key_rows.reshape(length, head_count, head_dim)
    value_heads = values.reshape(length, head_count, head_dim)

    def one_block(number):
        offset = number * block_size
        query_block = lax.dynamic_slice_in_dim(queries, offset, block_size, 0).reshape(
            block_size, head_count, head_dim
        )
        row_doc = lax.dynamic_slice_in_dim(segment, offset, block_size, 0)
        scores = (
            jnp.einsum("qhd,khd->hqk", query_block, key_heads, preferred_element_type=jnp.float32)
            * score_scale
        )
        masked = jnp.where((row_doc[:, None] == segment[None, :])[None], scores, mask_fill)
        row_peak = jnp.max(masked, axis=-1, keepdims=True)
        exponent = jnp.exp(masked - row_peak)
        row_total = jnp.sum(exponent, axis=-1, keepdims=True)
        soft_weights = (exponent / row_total).astype(jnp.bfloat16)
        attended = jnp.einsum(
            "hqk,khd->qhd", soft_weights, value_heads, preferred_element_type=jnp.float32
        )
        log_total = row_peak[..., 0] + jnp.log(row_total[..., 0])
        return (attended.reshape(block_size, model_width).astype(jnp.bfloat16), log_total)

    attended, log_total = lax.map(one_block, jnp.arange(length // block_size))
    return (attended.reshape(length, model_width), log_total)


def attention_backward(queries, key_rows, values, segment, log_total, grad_attended, head_dim):
    length, model_width = queries.shape
    head_count = model_width // head_dim
    block_size = min(block_rows, length)
    score_scale = float(head_dim) ** (-0.5)
    key_heads = key_rows.reshape(length, head_count, head_dim)
    value_heads = values.reshape(length, head_count, head_dim)

    def one_block(running, number):
        grad_key_sum, grad_value_sum = running
        offset = number * block_size
        query_block = lax.dynamic_slice_in_dim(queries, offset, block_size, 0).reshape(
            block_size, head_count, head_dim
        )
        grad_block = lax.dynamic_slice_in_dim(grad_attended, offset, block_size, 0).reshape(
            block_size, head_count, head_dim
        )
        row_doc = lax.dynamic_slice_in_dim(segment, offset, block_size, 0)
        row_log = log_total[number]
        scores = (
            jnp.einsum("qhd,khd->hqk", query_block, key_heads, preferred_element_type=jnp.float32)
            * score_scale
        )
        masked = jnp.where((row_doc[:, None] == segment[None, :])[None], scores, mask_fill)
        soft_weights = jnp.exp(masked - row_log[:, :, None])
        grad_soft = jnp.einsum(
            "qhd,khd->hqk", grad_block, value_heads, preferred_element_type=jnp.float32
        )
        row_inner = jnp.sum(soft_weights * grad_soft, axis=-1, keepdims=True)
        grad_scores = (soft_weights * (grad_soft - row_inner)).astype(jnp.bfloat16)
        grad_rows = (
            jnp.einsum("hqk,khd->qhd", grad_scores, key_heads, preferred_element_type=jnp.float32)
            * score_scale
        )
        grad_key_sum = (
            grad_key_sum
            + jnp.einsum(
                "hqk,qhd->khd", grad_scores, query_block, preferred_element_type=jnp.float32
            )
            * score_scale
        )
        grad_value_sum = grad_value_sum + jnp.einsum(
            "hqk,qhd->khd",
            soft_weights.astype(jnp.bfloat16),
            grad_block,
            preferred_element_type=jnp.float32,
        )
        return ((grad_key_sum, grad_value_sum), grad_rows.reshape(block_size, model_width))

    zero_heads = jnp.zeros((length, head_count, head_dim), jnp.float32)
    (grad_keys, grad_values), grad_rows = lax.scan(
        one_block, (zero_heads, zero_heads), jnp.arange(length // block_size)
    )
    return (
        grad_rows.reshape(length, model_width),
        grad_keys.reshape(length, model_width),
        grad_values.reshape(length, model_width),
    )


def forward_pack(token_rows, segment, weights, params, head_dim):
    attn_full, output_full, expand_full, reduce_full = weights
    down_reduced, up_low, projection_bias, hidden_unit_bias, norm_gain_rows, norm_shift_rows = (
        params
    )
    adapter_scale = adapter_alpha / down_reduced.shape[-1]
    adapter_rows = jnp.einsum(
        "td,gdr->gtr", token_rows, down_reduced, preferred_element_type=jnp.float32
    ).astype(jnp.bfloat16)
    projected = jnp.einsum("td,gde->gte", token_rows, attn_full, preferred_element_type=jnp.float32)
    lifted = jnp.einsum("gtr,grd->gtd", adapter_rows, up_low, preferred_element_type=jnp.float32)
    queries = (projected[0] + projection_bias[0] + adapter_scale * lifted[0]).astype(jnp.bfloat16)
    key_rows = projected[1].astype(jnp.bfloat16)
    values = (projected[2] + projection_bias[1] + adapter_scale * lifted[1]).astype(jnp.bfloat16)
    attended, log_total = attention_forward(queries, key_rows, values, segment, head_dim)
    pre_first = token_rows.astype(jnp.float32) + (
        matmul(attended, output_full) + projection_bias[2]
    )
    normed_first = layer_norm(pre_first, norm_gain_rows[0], norm_shift_rows[0])
    hidden = matmul(normed_first.astype(jnp.bfloat16), expand_full) + hidden_unit_bias
    active = gelu_exact(hidden).astype(jnp.bfloat16)
    pre_second = normed_first + (matmul(active, reduce_full) + projection_bias[3])
    final_output = layer_norm(pre_second, norm_gain_rows[1], norm_shift_rows[1]).astype(
        jnp.bfloat16
    )
    saved = (queries, key_rows, values, log_total, adapter_rows, pre_first, hidden, pre_second)
    return (final_output, saved)


def backward_pack(token_rows, segment, pack_cot, saved, weights, params, head_dim):
    attn_full, output_full, expand_full, reduce_full = weights
    down_reduced, up_low, projection_bias, hidden_unit_bias, norm_gain_rows, norm_shift_rows = (
        params
    )
    queries, key_rows, values, log_total, adapter_rows, pre_first, hidden, pre_second = saved
    adapter_scale = adapter_alpha / down_reduced.shape[-1]

    def norm_second(pre_values):
        return layer_norm(pre_values, norm_gain_rows[1], norm_shift_rows[1])

    def norm_first(pre_values):
        return layer_norm(pre_values, norm_gain_rows[0], norm_shift_rows[0])

    unused_second, second_pull = jax.vjp(norm_second, pre_second)
    grad_second = second_pull(pack_cot.astype(jnp.float32))[0]
    grad_active = matmul(grad_second.astype(jnp.bfloat16), reduce_full.T)
    unused_gelu, gelu_pull = jax.vjp(gelu_exact, hidden)
    grad_hidden = gelu_pull(grad_active)[0].astype(jnp.bfloat16)
    grad_normed = grad_second + matmul(grad_hidden, expand_full.T)
    unused_first, first_pull = jax.vjp(norm_first, pre_first)
    grad_first = first_pull(grad_normed)[0]
    grad_attended = matmul(grad_first.astype(jnp.bfloat16), output_full.T).astype(jnp.bfloat16)
    grad_queries, grad_keys, grad_values = attention_backward(
        queries, key_rows, values, segment, log_total, grad_attended, head_dim
    )
    grad_proj = jnp.stack([grad_queries, grad_keys, grad_values]).astype(jnp.bfloat16)
    adapted = jnp.stack([grad_proj[0], grad_proj[2]])
    grad_up = adapter_scale * jnp.einsum(
        "gtr,gtd->grd", adapter_rows, adapted, preferred_element_type=jnp.float32
    )
    grad_adapter = (
        adapter_scale
        * jnp.einsum("gtd,grd->gtr", adapted, up_low, preferred_element_type=jnp.float32)
    ).astype(jnp.bfloat16)
    grad_down = jnp.einsum(
        "td,gtr->gdr", token_rows, grad_adapter, preferred_element_type=jnp.float32
    )
    grad_tokens = grad_first + jnp.einsum(
        "gte,gde->td", grad_proj, attn_full, preferred_element_type=jnp.float32
    )
    grad_tokens = grad_tokens + jnp.einsum(
        "gtr,gdr->td", grad_adapter, down_reduced, preferred_element_type=jnp.float32
    )
    return (grad_tokens, grad_down, grad_up)


def flip(values, axis, bit, size):
    return lax.ppermute(values, axis, [(index, index ^ bit) for index in range(size)])


def butterfly_sum(values, sizes):
    for axis, size in sizes:
        if size & (size - 1):
            values = lax.psum(values, axis)
            continue
        bit = 1
        while bit < size:
            values = values + flip(values, axis, bit, size)
            bit *= 2
    return values


def shards(
    sizes,
    inputs,
    segments,
    cotangent,
    query_key_value_weight,
    attention_out_weight,
    feedforward_in_weight,
    feedforward_out_weight,
    projection_bias,
    hidden_unit_bias,
    norm_gain_rows,
    norm_shift_rows,
    adapter_down_factors,
    adapter_up_factors,
    down_first_moment,
    up_first_moment,
    down_second_moment,
    up_second_moment,
    optimizer_step_count,
):
    head_dim = HEAD_DIM
    weights = (
        lax.all_gather(query_key_value_weight, ("dp", "fsdp"), axis=1, tiled=True),
        lax.all_gather(attention_out_weight, ("dp", "fsdp"), axis=0, tiled=True),
        lax.all_gather(feedforward_in_weight, ("dp", "fsdp"), axis=0, tiled=True),
        lax.all_gather(feedforward_out_weight, ("dp", "fsdp"), axis=0, tiled=True),
    )
    params = (
        adapter_down_factors.astype(jnp.bfloat16),
        adapter_up_factors.astype(jnp.bfloat16),
        projection_bias,
        hidden_unit_bias,
        norm_gain_rows,
        norm_shift_rows,
    )

    def forward_step(unused, slices):
        final_output, saved = forward_pack(slices[0], slices[1], weights, params, head_dim)
        return (unused, (final_output, saved))

    unused_carry, (outputs, saved_all) = lax.scan(
        forward_step, jnp.zeros((), jnp.float32), (inputs, segments)
    )
    back_weights = (
        lax.all_gather(query_key_value_weight, ("dp", "fsdp"), axis=1, tiled=True),
        lax.all_gather(attention_out_weight, ("dp", "fsdp"), axis=0, tiled=True),
        lax.all_gather(feedforward_in_weight, ("dp", "fsdp"), axis=0, tiled=True),
        lax.all_gather(feedforward_out_weight, ("dp", "fsdp"), axis=0, tiled=True),
    )

    def backward_step(running, slices):
        token_rows, segment, pack_cot, saved = slices
        grad_tokens, grad_down, grad_up = backward_pack(
            token_rows, segment, pack_cot, saved, back_weights, params, head_dim
        )
        return ((running[0] + grad_down, running[1] + grad_up), grad_tokens)

    starting = (
        jnp.zeros(adapter_down_factors.shape, jnp.float32),
        jnp.zeros(adapter_up_factors.shape, jnp.float32),
    )
    (down_gradient_sum, up_gradient_sum), grad_inputs = lax.scan(
        backward_step, starting, (inputs, segments, cotangent, saved_all)
    )
    finished_steps = optimizer_step_count[0].astype(jnp.float32)
    packed = jnp.concatenate(
        [jnp.swapaxes(down_gradient_sum, 1, 2), up_gradient_sum], axis=0
    )
    packed = butterfly_sum(packed, sizes)
    down_grand_total = jnp.swapaxes(packed[:2], 1, 2)
    up_grand_total = packed[2:]
    grad_norm = jnp.sqrt(
        jnp.sum(down_grand_total * down_grand_total) + jnp.sum(up_grand_total * up_grand_total)
    )
    multiplier = jnp.minimum(1.0, clip_max / (grad_norm + 1e-06))
    revised_down, fresh_down_moment, fresh_down_square = adamw_update(
        adapter_down_factors,
        down_grand_total * multiplier,
        down_first_moment,
        down_second_moment,
        finished_steps,
        down_learning_rate,
        down_decay_factor,
    )
    revised_up, fresh_up_moment, fresh_up_square = adamw_update(
        adapter_up_factors,
        up_grand_total * multiplier,
        up_first_moment,
        up_second_moment,
        finished_steps,
        up_learning_rate,
        up_decay_factor,
    )
    return (
        outputs,
        grad_inputs,
        grad_norm,
        revised_down,
        revised_up,
        fresh_down_moment,
        fresh_up_moment,
        fresh_down_square,
        fresh_up_square,
    )


def solution(mesh):
    in_specs = (
        P(("dp", "fsdp"), None, None),
        P(("dp", "fsdp"), None),
        P(("dp", "fsdp"), None, None),
        P(None, ("dp", "fsdp"), None),
        P(("dp", "fsdp"), None),
        P(("dp", "fsdp"), None),
        P(("dp", "fsdp"), None),
        P(),
        P(),
        P(),
        P(),
        P(),
        P(),
        P(),
        P(),
        P(),
        P(),
        P(),
    )
    out_specs = (
        P(("dp", "fsdp"), None, None),
        P(("dp", "fsdp"), None, None),
        P(),
        P(),
        P(),
        P(),
        P(),
        P(),
        P(),
    )
    sizes = tuple((axis, mesh.shape[axis]) for axis in ("dp", "fsdp"))
    return jax.shard_map(functools.partial(shards, sizes), mesh=mesh, in_specs=in_specs, out_specs=out_specs, check_vma=False)
```
